256 devices in a mesh: row: 8 (over z), col: 32 (over x, y, core).
Axes of the slice: x: 4, y: 4, z: 8, core: 2. Of those that a mesh axis runs over, the one named last changes fastest.
Arguments:
- inputs: bfloat16 [768, 8192], P('col', 'row'), may hold values from -6 to 6
- out_grad: bfloat16 [768, 8192], P('col', 'row'), may hold values from -1.5 to 1.5
- w_gate: bfloat16 [8192, 28672], P('row', 'col'), may hold values from -0.0625 to 0.0625
- w_up: bfloat16 [8192, 28672], P('row', 'col'), may hold values from -0.0625 to 0.0625
- w_down: bfloat16 [28672, 8192], P('col', 'row'), may hold values from -0.03125 to 0.03125
Outputs:
- grad_inputs: bfloat16 [768, 8192], P('col', 'row')
- grad_wgate: bfloat16 [8192, 28672], P('row', 'col')
- grad_wup: bfloat16 [8192, 28672], P('row', 'col')
- grad_down: bfloat16 [28672, 8192], P('col', 'row')
The draws below stay inside these ranges and needn't reach their ends.
All inputs are finite; a program needn't handle non-finite values.
Results may differ from the reference program's by a relative error of at most 0.025.
Values may be sent and summed in bfloat16 or wider, within the bound.
No kernel may reach another device: no remote copies, remote signals or barrier semaphores. Data moves between devices by JAX's collectives and lax.ppermute only.
A program may use at most 64 MiB of HBM per device.

```python
import jax
import jax.numpy as jnp
from jax import lax

D = 8192
FF = 28672
TOKENS = 768
N_ROW = 8


def shard_levels(key, shape, split, least, top_value):
    loudness = 1.0
    for dim, parts in split:
        draws = jax.random.uniform(jax.random.fold_in(jax.random.fold_in(key, 6), dim), (parts,), jnp.float32, least / len(split), top_value / len(split))
        loudness = loudness * jnp.repeat(jnp.exp(draws), shape[dim] // parts).reshape((-1,) + (1,) * (len(shape) - 1 - dim))
    return loudness


def scatter_about(rng, dims, scale, limit, split=(), dtype=jnp.bfloat16):
    drawn = jax.random.normal(rng, dims, jnp.float32) * scale
    if len(split) > 0:
        drawn = shard_levels(rng, dims, split, -0.22, 0.18) * drawn
    return jnp.clip(drawn, min=-limit, max=limit).astype(dtype)


def setup_inputs(seed: int = 0) -> dict:
    key_of = jax.random.split(jax.random.key(seed), 6)
    return {
        "inputs": scatter_about(key_of[0], (TOKENS, D), 1.0, 6.0, ((0, 32), (1, 8))),
        "out_grad": scatter_about(key_of[1], (TOKENS, D), 0.25, 1.5, ((0, 32), (1, 8))),
        "w_gate": scatter_about(key_of[2], (D, FF), D ** -0.5, 0.0625, ((0, 8), (1, 32))),
        "w_up": scatter_about(key_of[3], (D, FF), D ** -0.5, 0.0625, ((0, 8), (1, 32))),
        "w_down": scatter_about(key_of[4], (FF, D), FF ** -0.5, 0.03125, ((0, 32), (1, 8))),
    }


def rounded(value):
    narrow = lax.optimization_barrier(value.astype(jnp.bfloat16))
    return narrow.astype(jnp.float32)


def reference(inputs, out_grad, w_gate, w_up, w_down):
    block_width = D // N_ROW
    gate = jnp.zeros((TOKENS, FF), jnp.float32)
    up = jnp.zeros((TOKENS, FF), jnp.float32)
    grad_hidden = jnp.zeros((TOKENS, FF), jnp.float32)
    for index_row in range(N_ROW):
        offset = index_row * block_width
        in_block = inputs[:, offset:offset + block_width]
        grad_block = out_grad[:, offset:offset + block_width]
        gate = gate + rounded(jnp.dot(in_block, w_gate[offset:offset + block_width], preferred_element_type=jnp.float32))
        up = up + rounded(jnp.dot(in_block, w_up[offset:offset + block_width], preferred_element_type=jnp.float32))
        grad_hidden = grad_hidden + rounded(lax.dot_general(grad_block, w_down[:, offset:offset + block_width], (((1,), (1,)), ((), ())), preferred_element_type=jnp.float32))
    squash = jax.nn.sigmoid(gate)
    activated = gate * squash
    hidden = (activated * up).astype(jnp.bfloat16)
    grad_gate = (grad_hidden * up * squash * (1.0 + gate * (1.0 - squash))).astype(jnp.bfloat16)
    grad_upact = (grad_hidden * activated).astype(jnp.bfloat16)
    token_contract = (((0,), (0,)), ((), ()))
    grad_down = lax.dot_general(hidden, out_grad, token_contract, preferred_element_type=jnp.float32).astype(jnp.bfloat16)
    grad_wgate = lax.dot_general(inputs, grad_gate, token_contract, preferred_element_type=jnp.float32).astype(jnp.bfloat16)
    grad_wup = lax.dot_general(inputs, grad_upact, token_contract, preferred_element_type=jnp.float32).astype(jnp.bfloat16)
    unit_contract = (((1,), (1,)), ((), ()))
    grad_inputs = lax.dot_general(grad_gate, w_gate, unit_contract, preferred_element_type=jnp.float32)
    grad_inputs = grad_inputs + lax.dot_general(grad_upact, w_up, unit_contract, preferred_element_type=jnp.float32)
    return (grad_inputs.astype(jnp.bfloat16), grad_wgate, grad_wup, grad_down)
```

```python
import jax
import jax.numpy as jnp
from jax import lax
from jax.sharding import PartitionSpec as P


BF16 = jnp.bfloat16
F32 = jnp.float32
SIDE = 4
RING = 8
pinned = lax.optimization_barrier


def along_row(value, hops):
    return pinned(lax.ppermute(value, "row", [(i, (i + hops) % RING) for i in range(RING)]))


def along_col(value, dx, dy, dcore):
    pairs = []
    for x in range(SIDE):
        for y in range(SIDE):
            for core in range(2):
                to = ((x + dx) % SIDE, (y + dy) % SIDE, core ^ dcore)
                pairs.append(((x * SIDE + y) * 2 + core, (to[0] * SIDE + to[1]) * 2 + to[2]))
    return pinned(lax.ppermute(value, "col", pairs))


def gather_tokens(value):
    value = jnp.concatenate(
        [value] + [along_col(value, -d, 0, 0) for d in range(1, SIDE)], axis=0
    )
    value = pinned(value)
    value = jnp.concatenate(
        [value] + [along_col(value, 0, -d, 0) for d in range(1, SIDE)], axis=0
    )
    value = pinned(value)
    return jnp.concatenate([value, along_col(value, 0, 0, 1)], axis=0)


def total_of(parts):
    result = parts[0].astype(F32)
    for part in parts[1:]:
        result = result + part.astype(F32)
    return result


def scatter_tokens(value):
    half = value.shape[0] // 2
    value = pinned(total_of([value[:half], along_col(value[half:], 0, 0, 1)]).astype(BF16))
    rows = half // SIDE
    value = pinned(
        total_of(
            [value[:rows]]
            + [along_col(value[d * rows : (d + 1) * rows], 0, d, 0) for d in range(1, SIDE)]
        ).astype(BF16)
    )
    rows = rows // SIDE
    return total_of(
        [value[:rows]]
        + [along_col(value[d * rows : (d + 1) * rows], d, 0, 0) for d in range(1, SIDE)]
    ).astype(BF16)


def scatter_ring(partial):
    here = lax.axis_index("row")
    rows = partial.shape[0] // RING
    half = rows // 2
    blocks = partial.reshape(RING, rows, partial.shape[1])

    def block(k):
        return lax.dynamic_index_in_dim(blocks, (here + k) % RING, 0, keepdims=False)

    def plus(a, b):
        return (a.astype(F32) + b.astype(F32)).astype(BF16)

    far = pinned(block(RING // 2))
    up = along_row(far[:half], 1)
    down = along_row(far[half:], -1)
    mine = block(3)
    up = along_row(pinned(jnp.concatenate([plus(mine[:half], up), mine[half:]], axis=0)), 1)
    mine = block(-3)
    down = along_row(pinned(jnp.concatenate([mine[:half], plus(mine[half:], down)], axis=0)), -1)
    for k in (2, 1):
        up = along_row(pinned(plus(block(k), up)), 1)
        down = along_row(pinned(plus(block(-k), down)), -1)
    return total_of([block(0), up, down])


def gather_ring(value):
    half = value.shape[0] // 2
    ups, downs = [value], [value]
    for _ in range(3):
        ups.append(along_row(ups[-1], 1))
        downs.append(along_row(downs[-1], -1))
    far = [along_row(ups[3][:half], 1), along_row(downs[3][half:], -1)]
    return jnp.concatenate([value, downs[1], downs[2], downs[3]] + far + ups[:0:-1], axis=0)


def rolled(value, start):
    double = jnp.concatenate([value, value], axis=0)
    return lax.dynamic_slice_in_dim(double, start, value.shape[0], 0)


def dot(a, b, contract):
    return lax.dot_general(a, b, (contract, ((), ())), preferred_element_type=F32)


def local(inputs, out_grad, w_gate, w_up, w_down):
    in_all = gather_tokens(inputs)
    grad_all = gather_tokens(out_grad)
    gate = scatter_ring(pinned(dot(in_all, w_gate, ((1,), (0,))).astype(BF16)))
    up = scatter_ring(pinned(dot(in_all, w_up, ((1,), (0,))).astype(BF16)))
    grad_hidden = scatter_ring(pinned(dot(grad_all, w_down, ((1,), (1,))).astype(BF16)))

    squash = jax.nn.sigmoid(gate)
    activated = gate * squash
    hidden = pinned((activated * up).astype(BF16))
    grad_gate = pinned(
        (grad_hidden * up * squash * (1.0 + gate * (1.0 - squash))).astype(BF16)
    )
    grad_upact = pinned((grad_hidden * activated).astype(BF16))

    gate_grads = gather_ring(grad_gate)
    up_grads = gather_ring(grad_upact)
    hidden_all = gather_ring(hidden)

    block = in_all.shape[0] // RING
    here = lax.axis_index("row")
    in_rolled = rolled(in_all, here * block)
    grad_rolled = rolled(grad_all, here * block)

    total = dot(gate_grads, w_gate, ((1,), (1,))) + dot(up_grads, w_up, ((1,), (1,)))
    total = rolled(total.astype(BF16), (RING - here) % RING * block)
    grad_inputs = scatter_tokens(total)
    grad_wgate = dot(in_rolled, gate_grads, ((0,), (0,))).astype(BF16)
    grad_wup = dot(in_rolled, up_grads, ((0,), (0,))).astype(BF16)
    grad_down = dot(hidden_all, grad_rolled, ((0,), (0,))).astype(BF16)
    return (grad_inputs, grad_wgate, grad_wup, grad_down)


def solution(mesh):
    return jax.shard_map(
        local,
        mesh=mesh,
        in_specs=(
            P("col", "row"),
            P("col", "row"),
            P("row", "col"),
            P("row", "col"),
            P("col", "row"),
        ),
        out_specs=(P("col", "row"), P("row", "col"), P("row", "col"), P("col", "row")),
        check_vma=False,
    )
```
